32 devices in a mesh: groups: 2 (over x), wide: 8 (over z, y), narrow: 2 (over core).
Axes of the slice: x: 2, y: 2, z: 4, core: 2. Of those that a mesh axis runs over, the one named last changes fastest.
Arguments:
- context_symbol_ids: int32 [2, 16, 16], P('narrow', 'groups'), parts along dimension 1, may hold values from 0 to 32767
- context_symbol_spans: int32 [2, 16], P('narrow', 'groups'), parts along dimension 1, may hold values from 1 to 16, as said below
- symbol_vector_lookup: bfloat16 [4096, 32768], P('wide'), may hold values from -6 to 6
- opening_lagged_blend: float32 [4096], replicated, may hold values from 0 to 1
- lagged_blend_weights: float32 [3, 4096], replicated, may hold values from 0 to 1
- blending_left_operand: bfloat16 [4096, 192], replicated, may hold values from -0.09375 to 0.09375
- blending_right_operands: bfloat16 [3, 64, 4096], replicated, may hold values from -0.375 to 0.375
- fixed_fading_scores: float32 [4096], P('wide'), may hold values from -6 to -1
- fading_left_operand: bfloat16 [4096, 128], replicated, may hold values from -0.09375 to 0.09375
- fading_right_operand: bfloat16 [128, 4096], P(None, 'wide'), may hold values from -0.5 to 0.5
- address_projector: bfloat16 [4096, 4096], P('wide'), may hold values from -0.09375 to 0.09375
- payload_projector: bfloat16 [4096, 4096], P('wide'), may hold values from -0.09375 to 0.09375
- present_symbol_reward: float32 [64, 64], replicated, may hold values from -1 to 1
- cluster_scaling_weight: float32 [4096], replicated, may hold values from 0.5 to 1.5
- cluster_scaling_offset: float32 [4096], replicated, may hold values from -3 to 3
- generated_acceptance: bfloat16 [2, 16, 4, 4096], P(None, ('groups', 'wide'), None, 'narrow'), parts along dimension 1, may hold values from -6 to 6
- generated_addresses: bfloat16 [2, 16, 4, 4096], P(None, ('groups', 'wide'), None, 'narrow'), parts along dimension 1, may hold values from -6 to 6
- generated_payloads: bfloat16 [2, 16, 4, 4096], P(None, ('groups', 'wide'), None, 'narrow'), parts along dimension 1, may hold values from -6 to 6
- generated_fading_scores: bfloat16 [2, 16, 4, 4096], P(None, ('groups', 'wide'), None, 'narrow'), parts along dimension 1, may hold values from -6 to -1
- generated_valve_scores: bfloat16 [2, 16, 4, 4096], P(None, ('groups', 'wide'), None, 'narrow'), parts along dimension 1, may hold values from -6 to 6
Outputs:
- dec_out: bfloat16 [2, 16, 4, 4096], P(None, ('groups', 'wide'), None, 'narrow'), parts along dimension 1
The draws below stay inside these ranges and needn't reach their ends.
There are 2 independent parts, one for each index of `groups`. The reference program is written for one: setup_inputs(seed, part) draws one part's arguments, and reference() takes and returns one part's arrays. A program takes and returns all parts, laid end to end along the dimension named above; an argument that names none is the same for every part. Nothing has to cross between parts.
Inputs may be any that keep to these rules, and one draw needn't show every extreme that they name: `context_symbol_spans`: positions at or past a prompt's length are padding. In every draw one of the 2 banks, chosen by the draw, holds only prompts of exactly 16 tokens, and every other bank holds at least one prompt of 16 tokens.
All inputs are finite; a program needn't handle non-finite values.
Results may differ from the reference program's by a relative error of at most 0.0095.
Values may be sent and summed in bfloat16 or wider, within the bound.
No kernel may reach another device: no remote copies, remote signals or barrier semaphores. Data moves between devices by JAX's collectives and lax.ppermute only.
A program may use at most 128 MiB of HBM per device.

```python
import jax
import jax.numpy as jnp
from jax import lax

ATTENDER_SUM = 64
WIDTH_OF_UNIT = 64
MIX = 64
DLORA = 128
V = 32768
L = 16
STEPS = 4
D = 4096
BANKS = 2
BANK_ROWS = 8


def full_bank(key):
    return jax.random.randint(jax.random.fold_in(key, 7), (), 0, BANKS)


def draw_context_symbol_spans(key, part):
    first_key, second_key = jax.random.split(jax.random.fold_in(key, 11))
    random_lengths = jax.random.randint(first_key, (BANKS, BANK_ROWS), 1, L + 1)
    chosen = jax.random.randint(second_key, (BANKS, 1), 0, BANK_ROWS)
    places = lax.broadcasted_iota(jnp.int32, (BANKS, BANK_ROWS), 1)
    ragged = jnp.where(places == chosen, L, random_lengths)
    banks = lax.broadcasted_iota(jnp.int32, (BANKS, BANK_ROWS), 0)
    return jnp.where(banks == full_bank(key), L, ragged).astype(jnp.int32)


def draw_context_symbol_ids(key, part):
    keys = jax.random.split(jax.random.fold_in(key, 23), 5)
    shape = (BANKS, BANK_ROWS, L)
    ceiling = jax.random.randint(keys[0], shape, 1, V + 1)
    ranks = jax.random.randint(keys[1], shape, 0, ceiling)
    common = jax.random.permutation(keys[2], jnp.arange(V, dtype=jnp.int32))[ranks]
    count = BANK_ROWS * L
    middle = jax.random.permutation(keys[3], jnp.arange(1, V - 1, dtype=jnp.int32))[:count - 2]
    ends = jnp.array([0, V - 1], jnp.int32)
    distinct = jax.random.permutation(keys[4], jnp.concatenate([ends, middle])).reshape(1, BANK_ROWS, L)
    banks = lax.broadcasted_iota(jnp.int32, (BANKS, 1, 1), 0)
    return jnp.where(banks == full_bank(key), distinct, common).astype(jnp.int32)


def block_scale(stream_key, dims, shards, low, top_value):
    def one(dim, blocks):
        heights = jax.random.uniform(jax.random.fold_in(jax.random.fold_in(stream_key, 6), dim), (blocks,), jnp.float32, low / len(shards), top_value / len(shards))
        return jnp.repeat(jnp.exp(heights), dims[dim] // blocks).reshape((-1,) + (1,) * (len(dims) - dim - 1))

    level = one(*shards[0])
    for cut in shards[1:]:
        level = level * one(*cut)
    return level


def noise(own_key, extent, scale, most, shards=(), held_as=jnp.bfloat16):
    factor_of = block_scale(own_key, extent, shards, -0.22, 0.18) if shards else 1.0
    values = jax.random.normal(own_key, extent, jnp.float32) * scale * factor_of
    return jnp.minimum(jnp.maximum(values, -most), most).astype(held_as)


def setup_inputs(seed: int = 0, part: int = 0) -> dict:
    key_list = jax.random.split(jax.random.key(seed), 21)
    own_keys = jax.random.split(jax.random.fold_in(key_list[20], part), 21)
    return {
        "context_symbol_ids": draw_context_symbol_ids(jax.random.fold_in(jax.random.fold_in(key_list[20], part), 71), part),
        "context_symbol_spans": draw_context_symbol_spans(jax.random.fold_in(jax.random.fold_in(key_list[20], part), 71), part),
        "symbol_vector_lookup": noise(key_list[2], (D, V), 1.0, 6.0, ((0, 8),)),
        "opening_lagged_blend": jnp.clip(jax.random.uniform(key_list[3], (D,), jnp.float32, 0.0, 1.0), 0.0, 1.0),
        "lagged_blend_weights": jnp.clip(jax.random.uniform(key_list[4], (3, D), jnp.float32, 0.0, 1.0), 0.0, 1.0),
        "blending_left_operand": noise(key_list[5], (D, 3 * MIX), D ** -0.5, 0.09375),
        "blending_right_operands": noise(key_list[6], (3, MIX, D), (4 * MIX) ** -0.5, 0.375),
        "fixed_fading_scores": jnp.clip(-6.0 + 5.0 * jax.random.uniform(key_list[7], (D,), jnp.float32) ** block_scale(key_list[7], (D,), ((0, 8),), -0.2, 0.2), -6.0, -1.0),
        "fading_left_operand": noise(key_list[8], (D, DLORA), D ** -0.5, 0.09375),
        "fading_right_operand": noise(key_list[9], (DLORA, D), DLORA ** -0.5, 0.5, ((1, 8),)),
        "address_projector": noise(key_list[10], (D, D), D ** -0.5, 0.09375, ((0, 8),)),
        "payload_projector": noise(key_list[11], (D, D), D ** -0.5, 0.09375, ((0, 8),)),
        "present_symbol_reward": jnp.clip(jax.random.uniform(key_list[12], (ATTENDER_SUM, WIDTH_OF_UNIT), jnp.float32, -1.0, 1.0), -1.0, 1.0),
        "cluster_scaling_weight": jnp.clip(jax.random.uniform(key_list[13], (D,), jnp.float32, 0.5, 1.5), 0.5, 1.5),
        "cluster_scaling_offset": noise(key_list[14], (D,), 0.5, 3.0, (), jnp.float32),
        "generated_acceptance": noise(own_keys[15], (BANKS, BANK_ROWS, STEPS, D), 1.0, 6.0, ((1, 8), (3, 2))),
        "generated_addresses": noise(own_keys[16], (BANKS, BANK_ROWS, STEPS, D), 1.0, 6.0, ((1, 8), (3, 2))),
        "generated_payloads": noise(own_keys[17], (BANKS, BANK_ROWS, STEPS, D), 1.0, 6.0, ((1, 8), (3, 2))),
        "generated_fading_scores": jnp.clip(-6.0 + 5.0 * jax.random.uniform(own_keys[18], (BANKS, BANK_ROWS, STEPS, D), jnp.float32) ** block_scale(own_keys[18], (BANKS, BANK_ROWS, STEPS, D), ((1, 8), (3, 2)), -0.2, 0.2), -6.0, -1.0).astype(jnp.bfloat16),
        "generated_valve_scores": noise(own_keys[19], (BANKS, BANK_ROWS, STEPS, D), 1.0, 6.0, ((1, 8), (3, 2))),
    }


norm_eps = 0.00064

def mix_project(embedded, opening_lagged_blend, lagged_blend_weights, blending_left_operand, blending_right_operands, fixed_fading_scores, fading_left_operand, fading_right_operand, address_projector, payload_projector):
    features = embedded.shape[2]
    previous = jnp.pad(embedded, ((0, 0), (1, 0), (0, 0)))[:, :-1, :]
    current = embedded.reshape(-1, features).astype(jnp.float32)
    difference = previous.reshape(-1, features).astype(jnp.float32) - current
    mixed_in = (current + difference * opening_lagged_blend).astype(jnp.bfloat16)
    hidden = jnp.tanh(jnp.dot(mixed_in, blending_left_operand, preferred_element_type=jnp.float32)).astype(jnp.bfloat16)
    rank_size = blending_right_operands.shape[1]
    branches = []
    for branch in range(3):
        shift_term = jnp.dot(hidden[:, branch * rank_size:(branch + 1) * rank_size], blending_right_operands[branch], preferred_element_type=jnp.float32)
        branches.append((current + difference * (lagged_blend_weights[branch] + shift_term)).astype(jnp.bfloat16))
    decay_hidden = jnp.tanh(jnp.dot(branches[0], fading_left_operand, preferred_element_type=jnp.float32)).astype(jnp.bfloat16)
    decay_log = fixed_fading_scores + jnp.dot(decay_hidden, fading_right_operand, preferred_element_type=jnp.float32)
    key_proj = jnp.dot(branches[1], address_projector.T, preferred_element_type=jnp.float32).astype(jnp.bfloat16)
    value_proj = jnp.dot(branches[2], payload_projector.T, preferred_element_type=jnp.float32).astype(jnp.bfloat16)
    return (key_proj, value_proj, decay_log)

def prefill_states(key_proj, value_proj, decay_log, lengths, attender_ordinal, attender_width):
    bank_count, bank_rows, length, features = key_proj.shape
    split_shape = (bank_count, bank_rows, length, attender_ordinal, attender_width)
    key_split = jnp.moveaxis(key_proj.astype(jnp.float32).reshape(split_shape), 2, 0)
    valued = jnp.moveaxis(value_proj.astype(jnp.float32).reshape(split_shape), 2, 0)
    factors = jnp.moveaxis(jnp.exp(-jnp.exp(decay_log)).reshape(split_shape), 2, 0)
    places = lax.iota(jnp.int32, length)
    live_mask = places[:, None, None] < lengths[None, :, :]

    def advance(recurrent_memories, inputs):
        present_address, present_payload, factor_now, live_now = inputs
        updated = factor_now[..., :, None] * recurrent_memories + present_address[..., :, None] * present_payload[..., None, :]
        return (jnp.where(live_now[:, :, None, None, None], updated, recurrent_memories), None)
    initial = jnp.zeros((bank_count, bank_rows, attender_ordinal, attender_width, attender_width), jnp.float32)
    recurrent_memories, unused = lax.scan(advance, initial, (key_split, valued, factors, live_mask))
    return recurrent_memories

def generation_iterations(recurrent_memories, acceptance_lines, address_source, payload_source, fading_source, valve_source, shard_reward, shard_scaling_weight, shard_scaling_offset):
    attender_ordinal = recurrent_memories.shape[-3]
    attender_width = recurrent_memories.shape[-1]
    leading = acceptance_lines.shape[:-2]
    step_count = acceptance_lines.shape[-2]
    split_shape = leading + (step_count, attender_ordinal, attender_width)
    receptance = acceptance_lines.astype(jnp.float32).reshape(split_shape)
    key_split = address_source.astype(jnp.float32).reshape(split_shape)
    valued = payload_source.astype(jnp.float32).reshape(split_shape)
    factors = jnp.exp(-jnp.exp(fading_source.astype(jnp.float32))).reshape(split_shape)
    results = []
    for position in range(step_count):
        present_acceptance = receptance[..., position, :, :]
        present_address = key_split[..., position, :, :]
        present_payload = valued[..., position, :, :]
        immediate_summand = lax.optimization_barrier(jnp.sum(present_acceptance * shard_reward * present_address, axis=-1, keepdims=True)) * present_payload
        carried = jnp.einsum('...hi,...hij->...hj', present_acceptance, recurrent_memories, precision=lax.Precision.HIGHEST)
        results.append(carried + immediate_summand)
        if position + 1 < step_count:
            recurrent_memories = factors[..., position, :, :][..., :, None] * recurrent_memories + present_address[..., :, None] * present_payload[..., None, :]
    mixed_out = jnp.stack(results, axis=-3)
    average = lax.optimization_barrier(jnp.mean(mixed_out, axis=-1, keepdims=True))
    centred = mixed_out - average
    spread = lax.optimization_barrier(jnp.mean(centred * centred, axis=-1, keepdims=True))
    normed = (centred * lax.rsqrt(spread + norm_eps)).reshape(leading + (step_count, attender_ordinal * attender_width))
    return ((normed * shard_scaling_weight + shard_scaling_offset) * jax.nn.silu(valve_source.astype(jnp.float32))).astype(jnp.bfloat16)

def reference(context_symbol_ids, context_symbol_spans, symbol_vector_lookup, opening_lagged_blend, lagged_blend_weights, blending_left_operand, blending_right_operands, fixed_fading_scores, fading_left_operand, fading_right_operand, address_projector, payload_projector, present_symbol_reward, cluster_scaling_weight, cluster_scaling_offset, generated_acceptance, generated_addresses, generated_payloads, generated_fading_scores, generated_valve_scores):
    bank_count, bank_rows, length = context_symbol_ids.shape
    features = symbol_vector_lookup.shape[0]
    attender_ordinal, attender_width = present_symbol_reward.shape
    picked = jnp.take(symbol_vector_lookup, context_symbol_ids.reshape(-1), axis=1)
    embedded = picked.T.reshape(bank_count * bank_rows, length, features)
    key_proj, value_proj, decay_log = mix_project(embedded, opening_lagged_blend, lagged_blend_weights, blending_left_operand, blending_right_operands, fixed_fading_scores, fading_left_operand, fading_right_operand, address_projector, payload_projector)
    shaped = (bank_count, bank_rows, length, features)
    recurrent_memories = prefill_states(key_proj.reshape(shaped), value_proj.reshape(shaped), decay_log.reshape(shaped), context_symbol_spans, attender_ordinal, attender_width)
    return generation_iterations(recurrent_memories, generated_acceptance, generated_addresses, generated_payloads, generated_fading_scores, generated_valve_scores, present_symbol_reward, cluster_scaling_weight, cluster_scaling_offset)
```

```python
import functools

import jax
import jax.numpy as jnp
from jax import lax
from jax.experimental import pallas as pl
from jax.experimental.pallas import tpu as pltpu
from jax.sharding import PartitionSpec as P

norm_eps = 0.00064
LANES = 128
bf16 = jnp.bfloat16
f32 = jnp.float32
NT = (((1,), (1,)), ((), ()))
VMEM = pl.BlockSpec(memory_space=pltpu.VMEM)
SMEM = pl.BlockSpec(memory_space=pltpu.SMEM)
ANY = pl.BlockSpec(memory_space=pl.ANY)


def dot(a, b):
    return jnp.dot(a, b, preferred_element_type=f32)


def dot_nt(a, b):
    return lax.dot_general(a, b, NT, preferred_element_type=f32)


def bf16_parts(x, count):
    parts = []
    for _ in range(count - 1):
        head = x.astype(bf16)
        parts.append(head)
        x = x - head.astype(f32)
    parts.append(x.astype(bf16))
    return parts


def pick_kernel(ids_ref, table_ref, out_ref, held, placed, sems, *, batch):
    tokens = held.shape[0]
    features = held.shape[1]
    batches = tokens // batch

    def copy(token):
        block = ids_ref[token] // LANES
        return pltpu.make_async_copy(
            table_ref.at[:, pl.ds(pl.multiple_of(block * LANES, LANES), LANES)],
            held.at[token],
            sems.at[token // batch],
        )

    def start(token, carry):
        copy(token).start()
        return carry

    lax.fori_loop(0, tokens, start, 0)
    rows = min(features, 64)
    lane = lax.broadcasted_iota(jnp.int32, (rows, LANES), 1)

    for group in range(batches):
        first = group * batch
        def wait(token, carry, first=first):
            copy(first + token).wait()
            return carry

        lax.fori_loop(0, batch, wait, 0)
        slot = first // LANES
        shifts = [
            jnp.remainder(first % LANES + k - ids_ref[first + k], LANES) for k in range(batch)
        ]

        def strip(step, carry, first=first, slot=slot, shifts=shifts):
            here = pl.ds(pl.multiple_of(step * rows, rows), rows)
            total = placed[slot, here, :]
            for k in range(batch):
                moved = pltpu.roll(held[first + k, here, :].astype(f32), shifts[k], 1)
                total = jnp.where(lane == first % LANES + k, moved, total)
            placed[slot, here, :] = total
            return carry

        lax.fori_loop(0, features // rows, strip, 0)
    for slot in range(placed.shape[0]):
        out_ref[slot * LANES : (slot + 1) * LANES, :] = placed[slot].T.astype(bf16)


def pick(table, ids):
    features = table.shape[0]
    tokens = ids.shape[0]
    batch = 16
    return pl.pallas_call(
        functools.partial(pick_kernel, batch=batch),
        out_shape=jax.ShapeDtypeStruct((tokens, features), bf16),
        in_specs=[SMEM, ANY],
        out_specs=VMEM,
        scratch_shapes=[
            pltpu.VMEM((tokens, features, LANES), bf16),
            pltpu.VMEM((tokens // LANES, features, LANES), f32),
            pltpu.SemaphoreType.DMA((tokens // batch,)),
        ],
        cost_estimate=pl.CostEstimate(
            flops=0, bytes_accessed=tokens * features * LANES * 2, transcendentals=0
        ),
        name="pick",
    )(ids, table)


def factor_kernel(
    owners_ref,
    spans_ref,
    *refs,
    blocks,
    width,
    length,
    rank,
):
    embeds = refs[:blocks]
    (
        opening_ref,
        lagged_ref,
        left_ref,
        right_ref,
        fixed_ref,
        decay_left_ref,
        decay_right_ref,
        key_ref,
        value_ref,
        out_ref,
        gap_ref,
    ) = refs[blocks:]
    rows = embeds[0].shape[0]
    places = lax.broadcasted_iota(jnp.int32, (rows, width), 0) % length
    first = places == 0
    strips = embeds[0].shape[1] // width

    def spots():
        for block in range(blocks):
            base = owners_ref[block] * embeds[block].shape[1]
            for strip in range(strips):
                column = base + strip * width
                where = pl.ds(pl.multiple_of(column, width), width)
                yield block * strips + strip, embeds[block], slice(strip * width, (strip + 1) * width), where

    hidden = None
    for index, ref, here, there in spots():
        current = ref[:, here].astype(f32)
        gap = jnp.where(first, 0.0, pltpu.roll(current, 1, 0)) - current
        gap_ref[:, index * width : (index + 1) * width] = gap
        mixed = (current + gap * opening_ref[:, there]).astype(bf16)
        part = dot_nt(mixed, left_ref[:, there])
        hidden = part if hidden is None else hidden + part
    hidden = jnp.tanh(hidden).astype(bf16)
    lows = [hidden[:, j * rank : (j + 1) * rank] for j in range(3)]
    sums = [None, None, None]
    for index, ref, here, there in spots():
        current = ref[:, here].astype(f32)
        gap = gap_ref[:, index * width : (index + 1) * width]
        for j in range(3):
            shift = lagged_ref[j : j + 1, there] + dot(lows[j], right_ref[j, :, there])
            branch = (current + gap * shift).astype(bf16)
            if j == 0:
                part = dot(branch, decay_left_ref[there, :])
            else:
                part = dot_nt(branch, (key_ref, value_ref)[j - 1][:, there])
            sums[j] = part if sums[j] is None else sums[j] + part
    decay_hidden = jnp.tanh(sums[0]).astype(bf16)
    decay_log = fixed_ref[...] + dot(decay_hidden, decay_right_ref[...])
    keys = sums[1].astype(bf16).astype(f32)
    values = sums[2].astype(bf16)
    rates = jnp.exp(decay_log)
    shape = (rows, rows)
    row = lax.broadcasted_iota(jnp.int32, shape, 0)
    column = lax.broadcasted_iota(jnp.int32, shape, 1)
    prompts = rows // length
    base = pl.program_id(0) * prompts
    span_of = jnp.zeros(shape, jnp.int32)
    for prompt in range(prompts):
        span_of = jnp.where(column // length == prompt, spans_ref[base + prompt], span_of)
    later = (row // length == column // length) & (column > row) & (column % length < span_of)
    later = jnp.where(later, 1.0, 0.0).astype(bf16)
    remaining = sum(dot(later, part) for part in bf16_parts(rates, 3))
    row_wide = lax.broadcasted_iota(jnp.int32, decay_log.shape, 0)
    span_wide = jnp.zeros(decay_log.shape, jnp.int32)
    for prompt in range(prompts):
        span_wide = jnp.where(row_wide // length == prompt, spans_ref[base + prompt], span_wide)
    weighted = jnp.where(row_wide % length < span_wide, keys * jnp.exp(-remaining), 0.0).astype(bf16)
    columns = weighted.shape[1]
    out_ref[:, 0:length, :] = weighted.reshape(prompts, length, columns)
    out_ref[:, length:, :] = values.reshape(prompts, length, columns)


def factors(
    embeds,
    owners,
    lengths,
    length,
    opening_lagged_blend,
    lagged_blend_weights,
    blending_left_operand,
    blending_right_operands,
    fixed_fading_scores,
    fading_left_operand,
    fading_right_operand,
    address_projector,
    payload_projector,
):
    tokens, block_width = embeds[0].shape
    features = address_projector.shape[1]
    columns = address_projector.shape[0]
    blocks = len(embeds)
    rows = length * max(1, min(LANES // length, tokens // length))
    width = min(block_width, 512)
    rank = blending_right_operands.shape[1]
    whole = lambda *shape: pl.BlockSpec(shape, lambda i: (0,) * len(shape))
    return pl.pallas_call(
        functools.partial(factor_kernel, blocks=blocks, width=width, length=length, rank=rank),
        grid=(tokens // rows,),
        out_shape=jax.ShapeDtypeStruct((tokens // length, 2 * length, columns), bf16),
        in_specs=[SMEM, SMEM]
        + [pl.BlockSpec((rows, block_width), lambda i: (i, 0)) for _ in embeds]
        + [
            whole(1, features),
            whole(3, features),
            whole(3 * rank, features),
            whole(3, rank, features),
            whole(1, columns),
            whole(*fading_left_operand.shape),
            whole(*fading_right_operand.shape),
            whole(columns, features),
            whole(columns, features),
        ],
        out_specs=pl.BlockSpec((rows // length, 2 * length, columns), lambda i: (i, 0, 0)),
        scratch_shapes=[pltpu.VMEM((rows, features), f32)],
        cost_estimate=pl.CostEstimate(
            flops=4 * tokens * features * columns,
            bytes_accessed=4 * features * columns,
            transcendentals=0,
        ),
        name="factors",
    )(
        owners,
        lengths,
        *embeds,
        opening_lagged_blend.reshape(1, -1),
        lagged_blend_weights,
        blending_left_operand.T,
        blending_right_operands,
        fixed_fading_scores.reshape(1, -1),
        fading_left_operand,
        fading_right_operand,
        address_projector,
        payload_projector,
    )


def head_sums(x, ones, parts):
    wide = ones.shape[0]
    return jnp.concatenate(
        [
            sum(dot(part, ones) for part in bf16_parts(x[:, k : k + wide], parts))
            for k in range(0, x.shape[1], wide)
        ],
        axis=1,
    )


def decode_kernel(
    bank_ref,
    own_ref,
    other_ref,
    receptance_ref,
    key_ref,
    value_ref,
    fading_ref,
    gate_ref,
    reward_ref,
    gain_ref,
    bias_ref,
    out_ref,
    *,
    head,
    length,
):
    steps = receptance_ref.shape[1]
    wide = 2 * LANES
    row = lax.broadcasted_iota(jnp.int32, (wide, wide), 0)
    column = lax.broadcasted_iota(jnp.int32, (wide, wide), 1)
    ones = jnp.where(row // head == column // head, 1.0, 0.0).astype(bf16)
    reward = reward_ref[...]
    for bank, ref in ((bank_ref[0], own_ref), (bank_ref[1], other_ref)):
        parcels = [ref[k] for k in range(ref.shape[0])]
        both = parcels[0] if len(parcels) == 1 else jnp.concatenate(parcels, axis=1)
        keys = both[0:length].astype(f32)
        values = both[length:].astype(f32)
        receptance = receptance_ref[bank].astype(f32)
        new_keys = key_ref[bank].astype(f32)
        new_values = value_ref[bank].astype(f32)
        factor = jnp.exp(-jnp.exp(fading_ref[bank].astype(f32)))
        gate = gate_ref[bank].astype(f32)
        results = []
        decay = None
        held = []
        for step in range(steps):
            now = receptance[step : step + 1]
            query = now if decay is None else now * decay
            score = head_sums(keys * query, ones, 2)
            fresh = [now * item for item in held]
            fresh.append(now * reward * new_keys[step : step + 1])
            fresh += [jnp.zeros_like(now)] * (steps - len(fresh))
            near = head_sums(jnp.concatenate(fresh, axis=0), ones, 2)
            results.append(
                jnp.sum(score * values, axis=0, keepdims=True)
                + jnp.sum(near * new_values, axis=0, keepdims=True)
            )
            fade = factor[step : step + 1]
            decay = fade if decay is None else decay * fade
            held = [item * fade for item in held] + [new_keys[step : step + 1]]
        mixed = jnp.concatenate(results, axis=0)
        centred = mixed - head_sums(mixed, ones, 3) * (1.0 / head)
        spread = head_sums(centred * centred, ones, 3) * (1.0 / head)
        normed = centred * lax.rsqrt(spread + norm_eps)
        out = (normed * gain_ref[...] + bias_ref[...]) * (gate / (1.0 + jnp.exp(-gate)))
        out_ref[bank] = out.astype(bf16)


def decode(banks, own, other, streams, reward, gain, bias, head, length):
    shape = streams[0].shape
    return pl.pallas_call(
        functools.partial(decode_kernel, head=head, length=length),
        out_shape=jax.ShapeDtypeStruct(shape, bf16),
        in_specs=[SMEM] + [VMEM] * 10,
        out_specs=VMEM,
        name="decode",
    )(banks, own, other, *streams, reward, gain, bias)


def per_device(
    context_symbol_ids,
    context_symbol_spans,
    symbol_vector_lookup,
    opening_lagged_blend,
    lagged_blend_weights,
    blending_left_operand,
    blending_right_operands,
    fixed_fading_scores,
    fading_left_operand,
    fading_right_operand,
    address_projector,
    payload_projector,
    present_symbol_reward,
    cluster_scaling_weight,
    cluster_scaling_offset,
    generated_acceptance,
    generated_addresses,
    generated_payloads,
    generated_fading_scores,
    generated_valve_scores,
):
    wide = lax.axis_size("wide")
    narrow = lax.axis_size("narrow")
    place = lax.axis_index("wide")
    core = lax.axis_index("narrow")
    length = context_symbol_ids.shape[2]
    columns = symbol_vector_lookup.shape[0]
    head = present_symbol_reward.shape[1]
    lengths = context_symbol_spans.reshape(-1)

    picked = pick(symbol_vector_lookup, context_symbol_ids.reshape(-1))
    if wide <= 16 and columns % LANES == 0:
        embeds = [picked]
        for shift in range(1, wide):
            embeds.append(
                lax.ppermute(picked, "wide", [(i, (i + shift) % wide) for i in range(wide)])
            )
        owners = jnp.remainder(place - jnp.arange(wide, dtype=jnp.int32), wide)
    else:
        gathered = lax.all_gather(picked, "wide", axis=0)
        embeds = [gathered.transpose(1, 0, 2).reshape(picked.shape[0], wide * columns)]
        owners = jnp.zeros((1,), jnp.int32)
    parcel = factors(
        embeds,
        owners,
        lengths,
        length,
        opening_lagged_blend,
        lagged_blend_weights,
        blending_left_operand,
        blending_right_operands,
        fixed_fading_scores,
        fading_left_operand,
        fading_right_operand,
        address_projector,
        payload_projector,
    )
    handed = lax.all_to_all(parcel, "wide", split_axis=0, concat_axis=0, tiled=True)
    share = wide // narrow
    own = lax.dynamic_slice_in_dim(handed, core * share, share, 0)
    away = lax.dynamic_slice_in_dim(handed, (1 - core) * share, share, 0)
    other = lax.ppermute(away, "narrow", [(0, 1), (1, 0)])
    if columns % LANES:
        own, other = (
            x.transpose(1, 0, 2).reshape(1, 2 * length, share * columns) for x in (own, other)
        )
    streams = [
        x.reshape(x.shape[0], x.shape[2], x.shape[3])
        for x in (
            generated_acceptance,
            generated_addresses,
            generated_payloads,
            generated_fading_scores,
            generated_valve_scores,
        )
    ]
    part = share * columns
    take = lambda x: lax.dynamic_slice_in_dim(x.reshape(1, -1), core * part, part, 1)
    out = decode(
        jnp.stack([core, 1 - core]).astype(jnp.int32),
        own,
        other,
        streams,
        take(present_symbol_reward),
        take(cluster_scaling_weight),
        take(cluster_scaling_offset),
        head,
        length,
    )
    return out.reshape(generated_acceptance.shape)


def solution(mesh):
    placed = (
        P("narrow", "groups", None),
        P("narrow", "groups"),
        P("wide", None),
        P(),
        P(),
        P(),
        P(),
        P("wide"),
        P(),
        P(None, "wide"),
        P("wide", None),
        P("wide", None),
        P(),
        P(),
        P(),
        P(None, ("groups", "wide"), None, "narrow"),
        P(None, ("groups", "wide"), None, "narrow"),
        P(None, ("groups", "wide"), None, "narrow"),
        P(None, ("groups", "wide"), None, "narrow"),
        P(None, ("groups", "wide"), None, "narrow"),
    )
    return jax.shard_map(
        per_device,
        mesh=mesh,
        in_specs=placed,
        out_specs=P(None, ("groups", "wide"), None, "narrow"),
        check_vma=False,
    )
```

```python
import functools

import jax
import jax.numpy as jnp
from jax import lax
from jax.experimental import pallas as pl
from jax.experimental.pallas import tpu as pltpu
from jax.sharding import PartitionSpec as P

norm_eps = 0.00064
LANES = 128
bf16 = jnp.bfloat16
f32 = jnp.float32
NT = (((1,), (1,)), ((), ()))
VMEM = pl.BlockSpec(memory_space=pltpu.VMEM)
SMEM = pl.BlockSpec(memory_space=pltpu.SMEM)
ANY = pl.BlockSpec(memory_space=pl.ANY)


def dot(a, b):
    return jnp.dot(a, b, preferred_element_type=f32)


def dot_nt(a, b):
    return lax.dot_general(a, b, NT, preferred_element_type=f32)


def bf16_parts(x, count):
    parts = []
    for _ in range(count - 1):
        head = x.astype(bf16)
        parts.append(head)
        x = x - head.astype(f32)
    parts.append(x.astype(bf16))
    return parts


def pick_kernel(ids_ref, table_ref, out_ref, held, placed, sems, *, batch, ahead):
    tokens, features, lanes = held.shape
    length = ids_ref.shape[1]
    batches = tokens // batch
    rows = min(features, 128)
    lane = lax.broadcasted_iota(jnp.int32, (rows, lanes), 1)

    def start(group):
        def one(step, carry):
            token = group * batch + step
            block = ids_ref[token // length, token % length] // lanes
            pltpu.make_async_copy(
                table_ref.at[:, pl.ds(pl.multiple_of(block * lanes, lanes), lanes)],
                held.at[token],
                sems.at[group],
            ).start()
            return carry

        lax.fori_loop(0, batch, one, 0)

    for group in range(min(ahead, batches)):
        start(group)
    for group in range(batches):
        first = group * batch
        slot = first // lanes
        here = held.at[pl.ds(first, batch)]
        pltpu.make_async_copy(here, here, sems.at[group]).wait()
        if group + ahead < batches:
            start(group + ahead)
        for strip in range(0, features, rows):
            total = placed[slot, strip : strip + rows, :]
            for step in range(batch):
                token = first + step
                target = token % lanes
                column = ids_ref[token // length, token % length] % lanes
                moved = pltpu.roll(
                    held[token, strip : strip + rows, :], jnp.remainder(target - column, lanes), 1
                )
                total = jnp.where(lane == target, moved, total)
            placed[slot, strip : strip + rows, :] = total
    for slot in range(placed.shape[0]):
        out_ref[slot * lanes : (slot + 1) * lanes, :] = placed[slot].T


def pick(table, ids):
    features = table.shape[0]
    tokens = ids.shape[0] * ids.shape[1]
    batch = 16
    size = tokens * features * LANES * 2
    return pl.pallas_call(
        functools.partial(pick_kernel, batch=batch, ahead=4),
        out_shape=jax.ShapeDtypeStruct((tokens, features), bf16),
        in_specs=[SMEM, ANY],
        out_specs=VMEM,
        scratch_shapes=[
            pltpu.VMEM((tokens, features, LANES), bf16),
            pltpu.VMEM((tokens // LANES, features, LANES), bf16),
            pltpu.SemaphoreType.DMA((tokens // batch,)),
        ],
        cost_estimate=pl.CostEstimate(flops=0, bytes_accessed=size, transcendentals=0),
        compiler_params=pltpu.CompilerParams(vmem_limit_bytes=size + (6 << 20)),
        name="pick",
    )(ids, table)


def factor_kernel(earlier_ref, spans_ref, *refs, offsets, single, width, length, rank):
    blocks = len(offsets)
    place = lax.axis_index("wide") if blocks > 1 else 0
    embeds = refs[:blocks]
    (
        opening_ref,
        lagged_ref,
        left_ref,
        right_ref,
        fixed_ref,
        decay_left_ref,
        decay_right_ref,
        key_ref,
        value_ref,
        out_ref,
        gap_ref,
    ) = refs[blocks:]
    rows = embeds[0].shape[0]
    places = lax.broadcasted_iota(jnp.int32, (rows, width), 0) % length
    first = places == 0
    strips = embeds[0].shape[1] // width

    def spots():
        for block in range(blocks):
            base = (place ^ offsets[block]) * embeds[block].shape[1] if blocks > 1 else 0
            for strip in range(strips):
                column = base + strip * width
                where = pl.ds(pl.multiple_of(column, width) if blocks > 1 else column, width)
                yield block * strips + strip, embeds[block], slice(strip * width, (strip + 1) * width), where

    hidden = None
    for index, ref, here, there in spots():
        current = ref[:, here].astype(f32)
        gap = jnp.where(first, 0.0, pltpu.roll(current, 1, 0)) - current
        gap_ref[:, index * width : (index + 1) * width] = gap
        mixed = (current + gap * opening_ref[:, there]).astype(bf16)
        part = dot_nt(mixed, left_ref[:, there])
        hidden = part if hidden is None else hidden + part
    hidden = jnp.tanh(hidden).astype(bf16)
    lows = [hidden[:, j * rank : (j + 1) * rank] for j in range(3)]
    sums = [None, None, None]
    for index, ref, here, there in spots():
        current = ref[:, here].astype(f32)
        gap = gap_ref[:, index * width : (index + 1) * width]
        for j in range(3):
            shift = lagged_ref[j : j + 1, there] + dot(lows[j], right_ref[j, :, there])
            branch = (current + gap * shift).astype(bf16)
            if j == 0:
                part = dot(branch, decay_left_ref[there, :])
            else:
                part = dot_nt(branch, (key_ref, value_ref)[j - 1][:, there])
            sums[j] = part if sums[j] is None else sums[j] + part
    decay_hidden = jnp.tanh(sums[0]).astype(bf16)
    decay_log = fixed_ref[...] + dot(decay_hidden, decay_right_ref[...])
    keys = sums[1].astype(bf16).astype(f32)
    values = sums[2].astype(bf16)
    rates = jnp.exp(decay_log)
    shape = (rows, rows)
    row = lax.broadcasted_iota(jnp.int32, shape, 0)
    column = lax.broadcasted_iota(jnp.int32, shape, 1)
    prompts = rows // length
    base = 0 if single else pl.program_id(0) * prompts
    span_of = jnp.zeros(shape, jnp.int32)
    for prompt in range(prompts):
        span_of = jnp.where(column // length == prompt, spans_ref[base + prompt], span_of)
    later = (row // length == column // length) & (column > row) & (column % length < span_of)
    later = jnp.where(later, 1.0, 0.0).astype(bf16)
    remaining = sum(dot(later, part) for part in bf16_parts(rates, 3))
    row_wide = lax.broadcasted_iota(jnp.int32, decay_log.shape, 0)
    span_wide = jnp.zeros(decay_log.shape, jnp.int32)
    for prompt in range(prompts):
        span_wide = jnp.where(row_wide // length == prompt, spans_ref[base + prompt], span_wide)
    weighted = jnp.where(row_wide % length < span_wide, keys * jnp.exp(-remaining), 0.0).astype(bf16)
    columns = weighted.shape[1]
    out_ref[:, 0:length, :] = weighted.reshape(prompts, length, columns)
    out_ref[:, length:, :] = values.reshape(prompts, length, columns)


def factors(
    earlier,
    embeds,
    offsets,
    lengths,
    length,
    opening_lagged_blend,
    lagged_blend_weights,
    blending_left_operand,
    blending_right_operands,
    fixed_fading_scores,
    fading_left_operand,
    fading_right_operand,
    address_projector,
    payload_projector,
):
    tokens, block_width = embeds[0].shape
    features = address_projector.shape[1]
    columns = address_projector.shape[0]
    rows = length * max(1, min(LANES // length, tokens // length))
    single = rows == tokens
    width = min(block_width, 512)
    rank = blending_right_operands.shape[1]
    weights = (
        opening_lagged_blend.reshape(1, -1),
        lagged_blend_weights,
        blending_left_operand.T,
        blending_right_operands,
        fixed_fading_scores.reshape(1, -1),
        fading_left_operand,
        fading_right_operand,
        address_projector,
        payload_projector,
    )
    out = jax.ShapeDtypeStruct((tokens // length, 2 * length, columns), bf16)
    if single:
        places = dict(in_specs=[ANY, SMEM] + [VMEM] * (len(embeds) + len(weights)), out_specs=VMEM)
        limit = 20 << 20
    else:
        kept = [pl.BlockSpec(x.shape, lambda i, rank=x.ndim: (0,) * rank) for x in weights]
        places = dict(
            grid=(tokens // rows,),
            in_specs=[ANY, SMEM]
            + [pl.BlockSpec((rows, block_width), lambda i: (i, 0)) for _ in embeds]
            + kept,
            out_specs=pl.BlockSpec((rows // length,) + out.shape[1:], lambda i: (i, 0, 0)),
        )
        limit = 48 << 20
    return pl.pallas_call(
        functools.partial(
            factor_kernel, offsets=offsets, single=single, width=width, length=length, rank=rank
        ),
        out_shape=out,
        scratch_shapes=[pltpu.VMEM((rows, features), f32)],
        cost_estimate=pl.CostEstimate(
            flops=4 * tokens * features * columns,
            bytes_accessed=4 * features * columns,
            transcendentals=0,
        ),
        compiler_params=pltpu.CompilerParams(vmem_limit_bytes=limit),
        name="factors",
        **places,
    )(earlier, lengths, *embeds, *weights)


def head_ones(wide, head):
    row = lax.broadcasted_iota(jnp.int32, (wide, wide), 0)
    column = lax.broadcasted_iota(jnp.int32, (wide, wide), 1)
    return jnp.where(row // head == column // head, 1.0, 0.0).astype(bf16)


def head_sums(x, ones, parts):
    wide = ones.shape[0]
    count = x.shape[0]
    tall = jnp.concatenate([x[:, k : k + wide] for k in range(0, x.shape[1], wide)], axis=0)
    total = sum(dot(part, ones) for part in bf16_parts(tall, parts))
    return jnp.concatenate(
        [total[k : k + count] for k in range(0, total.shape[0], count)], axis=1
    )


def local_kernel(
    receptance_ref,
    key_ref,
    value_ref,
    fading_ref,
    gate_ref,
    reward_ref,
    query_ref,
    near_ref,
    open_ref,
    *,
    head,
):
    banks, steps, width = receptance_ref.shape
    core = lax.axis_index("narrow")

    def flat(ref):
        return jnp.concatenate([ref[bank].astype(f32) for bank in range(banks)], axis=0)

    receptance, keys, values, gate = (
        flat(ref) for ref in (receptance_ref, key_ref, value_ref, gate_ref)
    )
    factor = jnp.exp(-jnp.exp(flat(fading_ref)))
    step = lax.broadcasted_iota(jnp.int32, receptance.shape, 0) % steps
    ones = head_ones(2 * LANES, head)
    reward = reward_ref[:, pl.ds(pl.multiple_of(core * width, LANES), width)]

    def earlier(x, count, fill):
        return jnp.where(step >= count, pltpu.roll(x, count, 0), fill)

    near = head_sums(receptance * reward * keys, ones, 3) * values
    query = receptance
    for count in range(1, steps):
        pair = query * earlier(keys, count, 0.0)
        near = near + head_sums(pair, ones, 3) * earlier(values, count, 0.0)
        query = query * earlier(factor, count, 1.0)
    query_ref[...] = query
    near_ref[...] = near
    open_ref[...] = gate / (1.0 + jnp.exp(-gate))


def local(streams, reward, head):
    banks, steps, width = streams[0].shape
    shape = jax.ShapeDtypeStruct((banks * steps, width), f32)
    return pl.pallas_call(
        functools.partial(local_kernel, head=head),
        out_shape=(shape,) * 3,
        in_specs=[VMEM] * 6,
        out_specs=(VMEM,) * 3,
        cost_estimate=pl.CostEstimate(
            flops=banks * steps * steps * width * 1000,
            bytes_accessed=banks * steps * width * 22,
            transcendentals=0,
        ),
        compiler_params=pltpu.CompilerParams(vmem_limit_bytes=8 << 20),
        name="local",
    )(*streams, reward)


def decode_kernel(
    handed_ref,
    other_ref,
    query_ref,
    near_ref,
    open_ref,
    gain_ref,
    bias_ref,
    out_ref,
    kept,
    tall,
    *,
    head,
    length,
):
    banks, steps, width = out_ref.shape
    share, _, columns = other_ref.shape
    core = lax.axis_index("narrow")
    for k in range(share):
        lanes = slice(k * columns, (k + 1) * columns)
        kept[core, :, lanes] = handed_ref[core * share + k].astype(f32)
        kept[1 - core, :, lanes] = other_ref[k].astype(f32)
    wide = 2 * LANES
    chunks = width // wide
    rows = banks * steps
    ones = head_ones(wide, head)
    query = query_ref[...]
    first = lax.broadcasted_iota(jnp.int32, query.shape, 0) < steps

    def line(place):
        return jnp.where(first, kept[0, place : place + 1, :], kept[1, place : place + 1, :])

    for place in range(0, length, 2):
        pair = jnp.concatenate([query * line(place), query * line(place + 1)], axis=0)
        for part, x in enumerate(bf16_parts(pair, 2)):
            for k in range(chunks):
                base = k * length * rows + place * rows
                tall[base : base + 2 * rows, part * wide : (part + 1) * wide] = x[
                    :, k * wide : (k + 1) * wide
                ]
    scores = dot(tall[...], jnp.concatenate([ones, ones], axis=0))
    mixed = near_ref[...]
    for place in range(length):
        base = [k * length * rows + place * rows for k in range(chunks)]
        score = jnp.concatenate([scores[b : b + rows] for b in base], axis=1)
        mixed = mixed + score * line(length + place)
    centred = mixed - head_sums(mixed, ones, 3) * (1.0 / head)
    spread = head_sums(centred * centred, ones, 3) * (1.0 / head)
    normed = centred * lax.rsqrt(spread + norm_eps)
    here = pl.ds(pl.multiple_of(core * width, LANES), width)
    out = ((normed * gain_ref[:, here] + bias_ref[:, here]) * open_ref[...]).astype(bf16)
    for bank in range(banks):
        out_ref[bank] = out[bank * steps : (bank + 1) * steps]


def decode(handed, other, prepared, gain, bias, shape, head, length):
    rows = shape[0] * shape[1]
    chunks = shape[2] // (2 * LANES)
    return pl.pallas_call(
        functools.partial(decode_kernel, head=head, length=length),
        out_shape=jax.ShapeDtypeStruct(shape, bf16),
        in_specs=[VMEM] * 7,
        out_specs=VMEM,
        scratch_shapes=[
            pltpu.VMEM((shape[0], 2 * length, shape[2]), f32),
            pltpu.VMEM((chunks * length * rows, 4 * LANES), bf16),
        ],
        compiler_params=pltpu.CompilerParams(vmem_limit_bytes=12 << 20),
        name="decode",
    )(handed, other, *prepared, gain, bias)


def gather_plan(wide):
    top = wide // 2
    plan = []
    for offset in sorted(range(1, wide), key=lambda o: (top < o < wide - 1, -(o == top), -(o == wide - 1))):
        if top < offset < wide - 1:
            plan.append((offset, top, offset ^ top))
        else:
            plan.append((offset, 0, offset))
    return plan


def per_device(
    context_symbol_ids,
    context_symbol_spans,
    symbol_vector_lookup,
    opening_lagged_blend,
    lagged_blend_weights,
    blending_left_operand,
    blending_right_operands,
    fixed_fading_scores,
    fading_left_operand,
    fading_right_operand,
    address_projector,
    payload_projector,
    present_symbol_reward,
    cluster_scaling_weight,
    cluster_scaling_offset,
    generated_acceptance,
    generated_addresses,
    generated_payloads,
    generated_fading_scores,
    generated_valve_scores,
):
    wide = lax.axis_size("wide")
    narrow = lax.axis_size("narrow")
    core = lax.axis_index("narrow")
    length = context_symbol_ids.shape[2]
    columns = symbol_vector_lookup.shape[0]
    head = present_symbol_reward.shape[1]
    lengths = context_symbol_spans.reshape(-1)

    streams = [
        x.reshape(x.shape[0], x.shape[2], x.shape[3])
        for x in (
            generated_acceptance,
            generated_addresses,
            generated_payloads,
            generated_fading_scores,
            generated_valve_scores,
        )
    ]
    picked = pick(symbol_vector_lookup, context_symbol_ids[0])
    weights = (
        opening_lagged_blend,
        lagged_blend_weights,
        blending_left_operand,
        blending_right_operands,
        fixed_fading_scores,
        fading_left_operand,
        fading_right_operand,
        address_projector,
        payload_projector,
    )
    if wide <= 16 and wide & (wide - 1) == 0 and columns % LANES == 0:
        held = {0: picked}
        for offset, source, hop in gather_plan(wide):
            held[offset] = lax.ppermute(
                held[source], "wide", [(i, i ^ hop) for i in range(wide)]
            )
        offsets = tuple(sorted(held))
        embeds = [held[offset] for offset in offsets]
    else:
        gathered = lax.all_gather(picked, "wide", axis=0)
        embeds = [gathered.transpose(1, 0, 2).reshape(picked.shape[0], wide * columns)]
        offsets = (0,)
    prepared = local(streams, present_symbol_reward.reshape(1, -1), head)
    parcel = factors(prepared[0], embeds, offsets, lengths, length, *weights)
    handed = lax.all_to_all(parcel, "wide", split_axis=0, concat_axis=0, tiled=True)
    share = wide // narrow
    away = lax.dynamic_slice_in_dim(handed, (1 - core) * share, share, 0)
    other = lax.ppermute(away, "narrow", [(0, 1), (1, 0)])
    if columns % LANES:
        handed = handed.reshape(narrow, share, 2 * length, columns).transpose(0, 2, 1, 3)
        handed = handed.reshape(narrow, 2 * length, share * columns)
        other = other.transpose(1, 0, 2).reshape(1, 2 * length, share * columns)
    out = decode(
        handed,
        other,
        prepared,
        cluster_scaling_weight.reshape(1, -1),
        cluster_scaling_offset.reshape(1, -1),
        streams[0].shape,
        head,
        length,
    )
    return out.reshape(generated_acceptance.shape)


def solution(mesh):
    placed = (
        P("narrow", "groups", None),
        P("narrow", "groups"),
        P("wide", None),
        P(),
        P(),
        P(),
        P(),
        P("wide"),
        P(),
        P(None, "wide"),
        P("wide", None),
        P("wide", None),
        P(),
        P(),
        P(),
        P(None, ("groups", "wide"), None, "narrow"),
        P(None, ("groups", "wide"), None, "narrow"),
        P(None, ("groups", "wide"), None, "narrow"),
        P(None, ("groups", "wide"), None, "narrow"),
        P(None, ("groups", "wide"), None, "narrow"),
    )
    return jax.shard_map(
        per_device,
        mesh=mesh,
        in_specs=placed,
        out_specs=P(None, ("groups", "wide"), None, "narrow"),
        check_vma=False,
    )
```

```python
import functools

import jax
import jax.numpy as jnp
from jax import lax
from jax.experimental import pallas as pl
from jax.experimental.pallas import tpu as pltpu
from jax.sharding import PartitionSpec as P

norm_eps = 0.00064
LANES = 128
bf16 = jnp.bfloat16
f32 = jnp.float32
NT = (((1,), (1,)), ((), ()))
VMEM = pl.BlockSpec(memory_space=pltpu.VMEM)
SMEM = pl.BlockSpec(memory_space=pltpu.SMEM)
ANY = pl.BlockSpec(memory_space=pl.ANY)


def dot(a, b):
    return jnp.dot(a, b, preferred_element_type=f32)


def dot_nt(a, b):
    return lax.dot_general(a, b, NT, preferred_element_type=f32)


def bf16_parts(x, count):
    parts = []
    for _ in range(count - 1):
        head = x.astype(bf16)
        parts.append(head)
        x = x - head.astype(f32)
    parts.append(x.astype(bf16))
    return parts


def pick_kernel(ids_ref, table_ref, out_ref, held, placed, sems, *, batch, ahead):
    tokens, features, lanes = held.shape
    length = ids_ref.shape[1]
    batches = tokens // batch
    rows = min(features, 128)
    lane = lax.broadcasted_iota(jnp.int32, (rows, lanes), 1)

    def start(group):
        def one(step, carry):
            token = group * batch + step
            block = ids_ref[token // length, token % length] // lanes
            pltpu.make_async_copy(
                table_ref.at[:, pl.ds(pl.multiple_of(block * lanes, lanes), lanes)],
                held.at[token],
                sems.at[group],
            ).start()
            return carry

        lax.fori_loop(0, batch, one, 0)

    for group in range(min(ahead, batches)):
        start(group)
    for group in range(batches):
        first = group * batch
        slot = first // lanes
        here = held.at[pl.ds(first, batch)]
        pltpu.make_async_copy(here, here, sems.at[group]).wait()
        if group + ahead < batches:
            start(group + ahead)
        for strip in range(0, features, rows):
            total = placed[slot, strip : strip + rows, :]
            for step in range(batch):
                token = first + step
                target = token % lanes
                column = ids_ref[token // length, token % length] % lanes
                moved = pltpu.roll(
                    held[token, strip : strip + rows, :], jnp.remainder(target - column, lanes), 1
                )
                total = jnp.where(lane == target, moved, total)
            placed[slot, strip : strip + rows, :] = total
    for slot in range(placed.shape[0]):
        out_ref[slot * lanes : (slot + 1) * lanes, :] = placed[slot].T


def pick(table, ids):
    features = table.shape[0]
    tokens = ids.shape[0] * ids.shape[1]
    batch = 16
    size = tokens * features * LANES * 2
    return pl.pallas_call(
        functools.partial(pick_kernel, batch=batch, ahead=4),
        out_shape=jax.ShapeDtypeStruct((tokens, features), bf16),
        in_specs=[SMEM, ANY],
        out_specs=VMEM,
        scratch_shapes=[
            pltpu.VMEM((tokens, features, LANES), bf16),
            pltpu.VMEM((tokens // LANES, features, LANES), bf16),
            pltpu.SemaphoreType.DMA((tokens // batch,)),
        ],
        cost_estimate=pl.CostEstimate(flops=0, bytes_accessed=size, transcendentals=0),
        compiler_params=pltpu.CompilerParams(vmem_limit_bytes=size + (6 << 20)),
        name="pick",
    )(ids, table)


def factor_kernel(spans_ref, *refs, offsets, single, width, length, rank):
    blocks = len(offsets)
    place = lax.axis_index("wide") if blocks > 1 else 0
    embeds = refs[:blocks]
    (
        opening_ref,
        lagged_ref,
        left_ref,
        right_ref,
        fixed_ref,
        decay_left_ref,
        decay_right_ref,
        key_ref,
        value_ref,
        out_ref,
        gap_ref,
    ) = refs[blocks:]
    rows = embeds[0].shape[0]
    places = lax.broadcasted_iota(jnp.int32, (rows, width), 0) % length
    first = places == 0
    strips = embeds[0].shape[1] // width

    def spots():
        for block in range(blocks):
            base = (place ^ offsets[block]) * embeds[block].shape[1] if blocks > 1 else 0
            for strip in range(strips):
                column = base + strip * width
                where = pl.ds(pl.multiple_of(column, width) if blocks > 1 else column, width)
                yield block * strips + strip, embeds[block], slice(strip * width, (strip + 1) * width), where

    hidden = None
    for index, ref, here, there in spots():
        current = ref[:, here].astype(f32)
        gap = jnp.where(first, 0.0, pltpu.roll(current, 1, 0)) - current
        gap_ref[:, index * width : (index + 1) * width] = gap
        mixed = (current + gap * opening_ref[:, there]).astype(bf16)
        part = dot_nt(mixed, left_ref[:, there])
        hidden = part if hidden is None else hidden + part
    hidden = jnp.tanh(hidden).astype(bf16)
    lows = [hidden[:, j * rank : (j + 1) * rank] for j in range(3)]
    sums = [None, None, None]
    for index, ref, here, there in spots():
        current = ref[:, here].astype(f32)
        gap = gap_ref[:, index * width : (index + 1) * width]
        for j in range(3):
            shift = lagged_ref[j : j + 1, there] + dot(lows[j], right_ref[j, :, there])
            branch = (current + gap * shift).astype(bf16)
            if j == 0:
                part = dot(branch, decay_left_ref[there, :])
            else:
                part = dot_nt(branch, (key_ref, value_ref)[j - 1][:, there])
            sums[j] = part if sums[j] is None else sums[j] + part
    decay_hidden = jnp.tanh(sums[0]).astype(bf16)
    decay_log = fixed_ref[...] + dot(decay_hidden, decay_right_ref[...])
    keys = sums[1].astype(bf16).astype(f32)
    values = sums[2].astype(bf16)
    rates = jnp.exp(decay_log)
    shape = (rows, rows)
    row = lax.broadcasted_iota(jnp.int32, shape, 0)
    column = lax.broadcasted_iota(jnp.int32, shape, 1)
    prompts = rows // length
    base = 0 if single else pl.program_id(0) * prompts
    span_of = jnp.zeros(shape, jnp.int32)
    for prompt in range(prompts):
        span_of = jnp.where(column // length == prompt, spans_ref[base + prompt], span_of)
    later = (row // length == column // length) & (column > row) & (column % length < span_of)
    later = jnp.where(later, 1.0, 0.0).astype(bf16)
    remaining = sum(dot(later, part) for part in bf16_parts(rates, 3))
    row_wide = lax.broadcasted_iota(jnp.int32, decay_log.shape, 0)
    span_wide = jnp.zeros(decay_log.shape, jnp.int32)
    for prompt in range(prompts):
        span_wide = jnp.where(row_wide // length == prompt, spans_ref[base + prompt], span_wide)
    weighted = jnp.where(row_wide % length < span_wide, keys * jnp.exp(-remaining), 0.0).astype(bf16)
    columns = weighted.shape[1]
    out_ref[:, 0:length, :] = weighted.reshape(prompts, length, columns)
    out_ref[:, length:, :] = values.reshape(prompts, length, columns)


def factors(
    embeds,
    offsets,
    lengths,
    length,
    opening_lagged_blend,
    lagged_blend_weights,
    blending_left_operand,
    blending_right_operands,
    fixed_fading_scores,
    fading_left_operand,
    fading_right_operand,
    address_projector,
    payload_projector,
):
    tokens, block_width = embeds[0].shape
    features = address_projector.shape[1]
    columns = address_projector.shape[0]
    rows = length * max(1, min(LANES // length, tokens // length))
    single = rows == tokens
    width = min(block_width, 512)
    rank = blending_right_operands.shape[1]
    weights = (
        opening_lagged_blend.reshape(1, -1),
        lagged_blend_weights,
        blending_left_operand.T,
        blending_right_operands,
        fixed_fading_scores.reshape(1, -1),
        fading_left_operand,
        fading_right_operand,
        address_projector,
        payload_projector,
    )
    out = jax.ShapeDtypeStruct((tokens // length, 2 * length, columns), bf16)
    if single:
        places = dict(in_specs=[SMEM] + [VMEM] * (len(embeds) + len(weights)), out_specs=VMEM)
        limit = 20 << 20
    else:
        kept = [pl.BlockSpec(x.shape, lambda i, rank=x.ndim: (0,) * rank) for x in weights]
        places = dict(
            grid=(tokens // rows,),
            in_specs=[SMEM]
            + [pl.BlockSpec((rows, block_width), lambda i: (i, 0)) for _ in embeds]
            + kept,
            out_specs=pl.BlockSpec((rows // length,) + out.shape[1:], lambda i: (i, 0, 0)),
        )
        limit = 48 << 20
    return pl.pallas_call(
        functools.partial(
            factor_kernel, offsets=offsets, single=single, width=width, length=length, rank=rank
        ),
        out_shape=out,
        scratch_shapes=[pltpu.VMEM((rows, features), f32)],
        cost_estimate=pl.CostEstimate(
            flops=4 * tokens * features * columns,
            bytes_accessed=4 * features * columns,
            transcendentals=0,
        ),
        compiler_params=pltpu.CompilerParams(vmem_limit_bytes=limit),
        name="factors",
        **places,
    )(lengths, *embeds, *weights)


def head_ones(wide, head):
    row = lax.broadcasted_iota(jnp.int32, (wide, wide), 0)
    column = lax.broadcasted_iota(jnp.int32, (wide, wide), 1)
    return jnp.where(row // head == column // head, 1.0, 0.0).astype(bf16)


def head_sums(x, ones, parts):
    wide = ones.shape[0]
    count = x.shape[0]
    tall = jnp.concatenate([x[:, k : k + wide] for k in range(0, x.shape[1], wide)], axis=0)
    total = sum(dot(part, ones) for part in bf16_parts(tall, parts))
    return jnp.concatenate(
        [total[k : k + count] for k in range(0, total.shape[0], count)], axis=1
    )


def local_kernel(
    receptance_ref,
    key_ref,
    value_ref,
    fading_ref,
    gate_ref,
    reward_ref,
    query_ref,
    near_ref,
    open_ref,
    *,
    head,
):
    banks, steps, width = receptance_ref.shape
    core = lax.axis_index("narrow")

    def flat(ref):
        return jnp.concatenate([ref[bank].astype(f32) for bank in range(banks)], axis=0)

    receptance, keys, values, gate = (
        flat(ref) for ref in (receptance_ref, key_ref, value_ref, gate_ref)
    )
    factor = jnp.exp(-jnp.exp(flat(fading_ref)))
    step = lax.broadcasted_iota(jnp.int32, receptance.shape, 0) % steps
    ones = head_ones(2 * LANES, head)
    reward = reward_ref[:, pl.ds(pl.multiple_of(core * width, LANES), width)]

    def earlier(x, count, fill):
        return jnp.where(step >= count, pltpu.roll(x, count, 0), fill)

    near = head_sums(receptance * reward * keys, ones, 3) * values
    query = receptance
    for count in range(1, steps):
        pair = query * earlier(keys, count, 0.0)
        near = near + head_sums(pair, ones, 3) * earlier(values, count, 0.0)
        query = query * earlier(factor, count, 1.0)
    query_ref[...] = query
    near_ref[...] = near
    open_ref[...] = gate / (1.0 + jnp.exp(-gate))


def local(streams, reward, head):
    banks, steps, width = streams[0].shape
    shape = jax.ShapeDtypeStruct((banks * steps, width), f32)
    return pl.pallas_call(
        functools.partial(local_kernel, head=head),
        out_shape=(shape,) * 3,
        in_specs=[VMEM] * 6,
        out_specs=(VMEM,) * 3,
        cost_estimate=pl.CostEstimate(
            flops=banks * steps * steps * width * 1000,
            bytes_accessed=banks * steps * width * 22,
            transcendentals=0,
        ),
        compiler_params=pltpu.CompilerParams(vmem_limit_bytes=8 << 20),
        name="local",
    )(*streams, reward)


def decode_kernel(
    handed_ref,
    other_ref,
    query_ref,
    near_ref,
    open_ref,
    gain_ref,
    bias_ref,
    out_ref,
    kept,
    tall,
    *,
    head,
    length,
):
    banks, steps, width = out_ref.shape
    share, _, columns = other_ref.shape
    core = lax.axis_index("narrow")
    for k in range(share):
        lanes = slice(k * columns, (k + 1) * columns)
        kept[core, :, lanes] = handed_ref[core * share + k].astype(f32)
        kept[1 - core, :, lanes] = other_ref[k].astype(f32)
    wide = 2 * LANES
    chunks = width // wide
    rows = banks * steps
    ones = head_ones(wide, head)
    query = query_ref[...]
    first = lax.broadcasted_iota(jnp.int32, query.shape, 0) < steps

    def line(place):
        return jnp.where(first, kept[0, place : place + 1, :], kept[1, place : place + 1, :])

    for place in range(0, length, 2):
        pair = jnp.concatenate([query * line(place), query * line(place + 1)], axis=0)
        for part, x in enumerate(bf16_parts(pair, 2)):
            for k in range(chunks):
                base = k * length * rows + place * rows
                tall[base : base + 2 * rows, part * wide : (part + 1) * wide] = x[
                    :, k * wide : (k + 1) * wide
                ]
    scores = dot(tall[...], jnp.concatenate([ones, ones], axis=0))
    mixed = near_ref[...]
    for place in range(length):
        base = [k * length * rows + place * rows for k in range(chunks)]
        score = jnp.concatenate([scores[b : b + rows] for b in base], axis=1)
        mixed = mixed + score * line(length + place)
    centred = mixed - head_sums(mixed, ones, 3) * (1.0 / head)
    spread = head_sums(centred * centred, ones, 3) * (1.0 / head)
    normed = centred * lax.rsqrt(spread + norm_eps)
    here = pl.ds(pl.multiple_of(core * width, LANES), width)
    out = ((normed * gain_ref[:, here] + bias_ref[:, here]) * open_ref[...]).astype(bf16)
    for bank in range(banks):
        out_ref[bank] = out[bank * steps : (bank + 1) * steps]


def decode(handed, other, prepared, gain, bias, shape, head, length):
    rows = shape[0] * shape[1]
    chunks = shape[2] // (2 * LANES)
    return pl.pallas_call(
        functools.partial(decode_kernel, head=head, length=length),
        out_shape=jax.ShapeDtypeStruct(shape, bf16),
        in_specs=[VMEM] * 7,
        out_specs=VMEM,
        scratch_shapes=[
            pltpu.VMEM((shape[0], 2 * length, shape[2]), f32),
            pltpu.VMEM((chunks * length * rows, 4 * LANES), bf16),
        ],
        compiler_params=pltpu.CompilerParams(vmem_limit_bytes=12 << 20),
        name="decode",
    )(handed, other, *prepared, gain, bias)


def gather_plan(wide):
    top = wide // 2
    plan = []
    for offset in sorted(range(1, wide), key=lambda o: (top < o < wide - 1, -(o == top), -(o == wide - 1))):
        if top < offset < wide - 1:
            plan.append((offset, top, offset ^ top))
        else:
            plan.append((offset, 0, offset))
    return plan


def per_device(
    context_symbol_ids,
    context_symbol_spans,
    symbol_vector_lookup,
    opening_lagged_blend,
    lagged_blend_weights,
    blending_left_operand,
    blending_right_operands,
    fixed_fading_scores,
    fading_left_operand,
    fading_right_operand,
    address_projector,
    payload_projector,
    present_symbol_reward,
    cluster_scaling_weight,
    cluster_scaling_offset,
    generated_acceptance,
    generated_addresses,
    generated_payloads,
    generated_fading_scores,
    generated_valve_scores,
):
    wide = lax.axis_size("wide")
    narrow = lax.axis_size("narrow")
    core = lax.axis_index("narrow")
    length = context_symbol_ids.shape[2]
    columns = symbol_vector_lookup.shape[0]
    head = present_symbol_reward.shape[1]
    lengths = context_symbol_spans.reshape(-1)

    streams = [
        x.reshape(x.shape[0], x.shape[2], x.shape[3])
        for x in (
            generated_acceptance,
            generated_addresses,
            generated_payloads,
            generated_fading_scores,
            generated_valve_scores,
        )
    ]
    ids = pltpu.with_memory_space_constraint(context_symbol_ids[0], pltpu.HBM)
    picked = pick(symbol_vector_lookup, ids)
    weights = (
        opening_lagged_blend,
        lagged_blend_weights,
        blending_left_operand,
        blending_right_operands,
        fixed_fading_scores,
        fading_left_operand,
        fading_right_operand,
        address_projector,
        payload_projector,
    )
    if wide <= 16 and wide & (wide - 1) == 0 and columns % LANES == 0:
        held = {0: picked}
        for offset, source, hop in gather_plan(wide):
            held[offset] = lax.ppermute(
                held[source], "wide", [(i, i ^ hop) for i in range(wide)]
            )
        offsets = tuple(sorted(held))
        embeds = [held[offset] for offset in offsets]
    else:
        gathered = lax.all_gather(picked, "wide", axis=0)
        embeds = [gathered.transpose(1, 0, 2).reshape(picked.shape[0], wide * columns)]
        offsets = (0,)
    prepared = local(streams, present_symbol_reward.reshape(1, -1), head)
    parcel = factors(embeds, offsets, lengths, length, *weights)
    handed = lax.all_to_all(parcel, "wide", split_axis=0, concat_axis=0, tiled=True)
    share = wide // narrow
    away = lax.dynamic_slice_in_dim(handed, (1 - core) * share, share, 0)
    other = lax.ppermute(away, "narrow", [(0, 1), (1, 0)])
    if columns % LANES:
        handed = handed.reshape(narrow, share, 2 * length, columns).transpose(0, 2, 1, 3)
        handed = handed.reshape(narrow, 2 * length, share * columns)
        other = other.transpose(1, 0, 2).reshape(1, 2 * length, share * columns)
    out = decode(
        handed,
        other,
        prepared,
        cluster_scaling_weight.reshape(1, -1),
        cluster_scaling_offset.reshape(1, -1),
        streams[0].shape,
        head,
        length,
    )
    return out.reshape(generated_acceptance.shape)


def solution(mesh):
    placed = (
        P("narrow", "groups", None),
        P("narrow", "groups"),
        P("wide", None),
        P(),
        P(),
        P(),
        P(),
        P("wide"),
        P(),
        P(None, "wide"),
        P("wide", None),
        P("wide", None),
        P(),
        P(),
        P(),
        P(None, ("groups", "wide"), None, "narrow"),
        P(None, ("groups", "wide"), None, "narrow"),
        P(None, ("groups", "wide"), None, "narrow"),
        P(None, ("groups", "wide"), None, "narrow"),
        P(None, ("groups", "wide"), None, "narrow"),
    )
    return jax.shard_map(
        per_device,
        mesh=mesh,
        in_specs=placed,
        out_specs=P(None, ("groups", "wide"), None, "narrow"),
        check_vma=False,
    )
```
